512 devices in a mesh: pair: 64 (over z, y), virt: 8 (over x, core).
Axes of the slice: x: 4, y: 4, z: 16, core: 2. Of those that a mesh axis runs over, the one named last changes fastest.
Arguments:
- amplitudes: bfloat16 [512, 8, 4096], P('pair', 'virt'), may hold values from -6 to 6
- partner: int32 [512], P('pair'), may hold values from 0 to 511, as said below
- integrals: bfloat16 [64, 4096, 4096], P('virt', 'pair'), may hold values from -0.09375 to 0.09375
- pattern: int32 [64], P('virt'), may hold values from 0 to 15, as said below
- owner: int32 [16], replicated, may hold values from 0 to 15, as said below
Outputs:
- ladder: bfloat16 [512, 16, 4096], P('pair', 'virt')
The draws below stay inside these ranges and needn't reach their ends.
Inputs may be any that keep to these rules, and one draw needn't show every extreme that they name: partner pairs each pair with another one and is its own inverse; the partner of a pair held by index j of pair is held by index j + 64 / 2 modulo 64, that is half the pair axis away. `pattern`: every ab tile pair appears exactly four times in all. owner names every ab tile pair exactly once.
All inputs are finite; a program needn't handle non-finite values.
Results may differ from the reference program's by a relative error of at most 0.0051.
Values may be sent and summed in bfloat16 or wider, within the bound.
A program may use at most 64 MiB of HBM per device.

```python
import jax
import jax.numpy as jnp
from jax import lax

TILE = 64
TT = 4096
PAIR_DEV = 8
NNZ_DEV = 8
PAIRS = 512
NAB = 16
N_PAIR = 64
N_VIRT = 8


def draw_partner(key, part):
    half = N_PAIR // 2
    keys = jax.random.split(jax.random.fold_in(key, 11), half)
    perms = jax.vmap(lambda one: jax.random.permutation(one, PAIR_DEV))(keys).astype(jnp.int32)
    inverse = jnp.argsort(perms, axis=1, stable=True).astype(jnp.int32)
    blocks = jnp.arange(half, dtype=jnp.int32)[:, None]
    lower = (blocks + half) * PAIR_DEV + perms
    upper = blocks * PAIR_DEV + inverse
    return jnp.concatenate([lower.reshape(-1), upper.reshape(-1)]).astype(jnp.int32)


def draw_pattern(key, part):
    total = N_VIRT * NNZ_DEV
    slots = jnp.arange(total, dtype=jnp.int32) % NAB
    shuffle = jax.random.permutation(jax.random.fold_in(key, 23), total).astype(jnp.int32)
    return jnp.take(slots, shuffle).astype(jnp.int32)


def draw_owner(key, part):
    return jax.random.permutation(jax.random.fold_in(key, 37), NAB).astype(jnp.int32)


def block_levels(own_key, dims, pieces, smallest, high):
    gain = 1.0
    for dim, blocks in pieces:
        draws = jax.random.uniform(jax.random.fold_in(jax.random.fold_in(own_key, 6), dim), (blocks,), jnp.float32, smallest / len(pieces), high / len(pieces))
        gain = gain * jnp.repeat(jnp.exp(draws), dims[dim] // blocks).reshape((-1,) + (1,) * (len(dims) - 1 - dim))
    return gain


def bell_draw(key, shape, deviation, reach, pieces=(), kind=jnp.bfloat16):
    factor_of = block_levels(key, shape, pieces, -0.22, 0.18) if pieces else 1.0
    drawn = jax.random.normal(key, shape, jnp.float32) * deviation * factor_of
    return jnp.minimum(jnp.maximum(drawn, -reach), reach).astype(kind)


def setup_inputs(seed: int = 0) -> dict:
    streams_of = jax.random.split(jax.random.key(seed), 6)
    amplitudes = bell_draw(streams_of[0], (PAIRS, N_VIRT, TT), 1.0, 6.0, ((0, 64), (1, 8)))
    partner = draw_partner(jax.random.fold_in(streams_of[5], 71), 0)
    integrals = bell_draw(streams_of[2], (N_VIRT * NNZ_DEV, TT, TT), TT ** -0.5, 0.09375, ((0, 8), (1, 64)))
    pattern = draw_pattern(jax.random.fold_in(streams_of[5], 71), 0)
    owner = draw_owner(jax.random.fold_in(streams_of[5], 71), 0)
    return dict(amplitudes=amplitudes, partner=partner, integrals=integrals, pattern=pattern, owner=owner)


def reference(amplitudes, partner, integrals, pattern, owner):
    mirror = jnp.take(amplitudes, partner, axis=0).reshape(PAIRS, N_VIRT, TILE, TILE)
    mirror = jnp.swapaxes(mirror, 2, 3).reshape(PAIRS, N_VIRT, TT)
    symmetric = (amplitudes.astype(jnp.float32) + mirror.astype(jnp.float32)).astype(jnp.bfloat16)

    def add_tile(total, index):
        column = (index // NNZ_DEV).astype(jnp.int32)
        left = lax.dynamic_index_in_dim(symmetric, column, axis=1, keepdims=False)
        right = lax.dynamic_index_in_dim(integrals, index, axis=0, keepdims=False)
        term = jnp.dot(left, right.T, preferred_element_type=jnp.float32)
        target = pattern[index].astype(jnp.int32)
        current = lax.dynamic_index_in_dim(total, target, axis=1, keepdims=False)
        total = lax.dynamic_update_index_in_dim(total, current + term, target, 1)
        return total, None

    summed = jnp.zeros((PAIRS, NAB, TT), jnp.float32)
    summed, unused = lax.scan(add_tile, summed, jnp.arange(N_VIRT * NNZ_DEV, dtype=jnp.int32))
    return jnp.take(summed, owner, axis=1).astype(jnp.bfloat16)
```

```python
import jax
import jax.numpy as jnp
from jax import lax
from jax.experimental import pallas as pl
from jax.experimental.pallas import tpu as pltpu
from jax.sharding import PartitionSpec as P

MESH = pl.DeviceIdType.MESH
NZ, NY, NX = 16, 4, 4
ROWS = 8
TT = 4096
CUT = 1280
HALF = (TT - CUT) // 2
ORDER = (4, 12, 3, 13, 5, 11, 2, 14, 6, 10, 1, 15, 7, 9, 0, 8)
GROUPS = {4: (0, 2), 5: (2, 6), 6: (6, 10), 7: (10, 14), 8: (14, 16)}

ACOLS = pl.ds(0, CUT)
BCOLS = pl.ds(CUT, TT - CUT)
BHALF = {1: pl.ds(CUT, HALF), -1: pl.ds(CUT + HALF, HALF)}
AHALF = {1: pl.ds(0, CUT // 2), -1: pl.ds(CUT // 2, CUT // 2)}


def kernel(amp, ints, partner, pattern, owner, out, gath, tile, flip, acc, perm, masks,
           one_out, one_own, one_in, two_out, two_in, final, landed, load_sem, send, recv):
    pair = lax.axis_index("pair")
    virt = lax.axis_index("virt")
    z, y = pair // NY, pair % NY
    x, core = virt // 2, virt % 2

    def at(dz, dy):
        return ((z + (dz % NZ)) % NZ * NY + (y + (dy % NY)) % NY, virt)

    def beside(dx, swap):
        return (pair, (x + dx) % NX * 2 + (1 - core if swap else core))

    load = pltpu.make_async_copy(ints, tile, load_sem)
    load.start()

    counter = [0]
    table = {}

    def message(key, src, dst, device):
        if key not in table:
            slot = counter[0]
            counter[0] += 1
            table[key] = pltpu.make_async_remote_copy(
                src_ref=src, dst_ref=dst, send_sem=send.at[slot], recv_sem=recv.at[slot],
                device_id=device, device_id_type=MESH)
        return table[key]

    def z_b(s, way):
        cols = BHALF[way] if s == 8 else BCOLS
        return message(("zb", s, way), gath.at[(-way * (s - 1)) % NZ, 0, :, cols],
                       gath.at[(-way * s) % NZ, 0, :, cols], at(way, 0))

    def z_a(s, way, dy):
        return message(("za", s, way, dy), gath.at[(-way * (s - 1)) % NZ, dy, :, ACOLS],
                       gath.at[(-way * s) % NZ, dy, :, ACOLS], at(way, 0))

    def y_b(dz, way):
        dz %= NZ
        return message(("yb", dz, way), gath.at[dz, 0, :, BCOLS], gath.at[dz, -way % NY, :, BCOLS], at(0, way))

    def y_b2(dz, way):
        dz %= NZ
        return message(("yb2", dz, way), gath.at[dz, -way % NY, :, BHALF[way]], gath.at[dz, 2, :, BHALF[way]], at(0, way))

    def y_a(way):
        return message(("ya", way), gath.at[0, 0, :, ACOLS], gath.at[0, -way % NY, :, ACOLS], at(0, way))

    def y_a2(way):
        return message(("ya2", way), gath.at[0, -way % NY, :, AHALF[way]], gath.at[0, 2, :, AHALF[way]], at(0, way))

    def stage_one(step):
        lo, hi = GROUPS[step]
        return message(("one", step), one_out.at[:, lo:hi], one_in.at[:, lo:hi], beside(0, True))

    def stage_two(step, dx):
        lo, hi = GROUPS[step]
        return message(("two", step, dx), two_out.at[dx - 1, lo:hi], two_in.at[dx - 1, lo:hi], beside(dx, False))

    def deliver(position, dy):
        return message(("out", position, dy), final.at[position, dy], landed.at[pair], at(ORDER[position], dy))

    rows_iota = lax.broadcasted_iota(jnp.int32, (ROWS, 1), 0)
    lower = z < NZ // 2
    place = [jnp.where(lower, r, partner[r] % ROWS) for r in range(ROWS)]
    plain = amp[...].astype(jnp.float32)
    sorted_rows = jnp.zeros((ROWS, TT), jnp.float32)
    for r in range(ROWS):
        sorted_rows = jnp.where(rows_iota == place[r], plain[r:r + 1, :], sorted_rows)
    gath[0, 0] = sorted_rows.astype(jnp.bfloat16)

    barrier = pltpu.get_barrier_semaphore()
    friends = [at(1, 0), at(-1, 0), at(0, 1), at(0, -1), beside(0, True), beside(1, False), beside(2, False), beside(3, False)]
    for friend in friends:
        pl.semaphore_signal(barrier, inc=1, device_id=friend, device_id_type=MESH)

    lanes = lax.broadcasted_iota(jnp.int32, (1, 128), 1)
    for dx in range(NX):
        for c in range(2):
            to = (x + dx) % NX * 2 + (core if c == 0 else 1 - core)
            first, second = owner[2 * to], owner[2 * to + 1]
            for kk in range(4):
                even, odd = pattern[2 * kk], pattern[2 * kk + 1]

                def hit(tile_id, slot_id):
                    return jnp.where(tile_id == slot_id, jnp.float32(1), jnp.float32(0))

                masks[dx * 2 + c, pl.ds(2 * kk, 1), :] = jnp.where(lanes < 64, hit(even, first), hit(odd, second))
                masks[dx * 2 + c, pl.ds(2 * kk + 1, 1), :] = jnp.where(lanes < 64, hit(odd, first), hit(even, second))

    pl.semaphore_wait(barrier, len(friends))

    for way in (1, -1):
        z_b(1, way).start()
        y_a(way).start()
    for way in (1, -1):
        z_a(1, way, 0).start()
    for way in (1, -1):
        y_b(0, way).start()

    row = lax.broadcasted_iota(jnp.int32, (512, 512), 0)
    col = lax.broadcasted_iota(jnp.int32, (512, 512), 1)
    perm[...] = jnp.where(col == (row % 8) * 64 + row // 8, 1.0, 0.0).astype(jnp.bfloat16)
    load.wait()

    def flip_block(i):
        parts = []
        for h in range(2):
            cols = pl.ds(i * 1024 + h * 512, 512)
            turned = lax.dot_general(perm[...], tile[:, cols], (((1,), (1,)), ((), ())), preferred_element_type=jnp.float32)
            parts.append(turned.reshape(64, 8, 512))
        flip[:, pl.ds(i * 16, 16), :] = jnp.concatenate(parts, axis=1).astype(jnp.bfloat16)

    written = set()

    def compute(dzs, n):
        dzs = [dz % NZ for dz in dzs]
        left = jnp.concatenate([gath[dz].reshape(NY * ROWS, TT) for dz in dzs], axis=0)
        if n < 2:
            right = tile[pl.ds(n * 256, 256), :]
            got = lax.dot_general(left, right, (((1,), (1,)), ((), ())), preferred_element_type=jnp.float32)
        else:
            right = flip[:, :, pl.ds((n - 2) * 256, 256)].reshape(TT, 256)
            got = jnp.dot(left, right, preferred_element_type=jnp.float32)
        cols = pl.ds(n % 2 * 256, 256)
        for i, dz in enumerate(dzs):
            goal = dz if n < 2 else (dz + 8) % NZ
            value = got[i * 32:(i + 1) * 32]
            if (goal, n % 2) in written:
                acc[goal, :, cols] += value
            else:
                written.add((goal, n % 2))
                acc[goal, :, cols] = value

    def spread(step):
        lo, hi = GROUPS[step]
        for position in range(lo, hi):
            dz = ORDER[position]
            straight = [acc[dz, :, pl.ds(128 * kk, 128)] for kk in range(4)]
            turned = [pltpu.roll(v, 64, 1) for v in straight]
            for dx in range(NX):
                for c in range(2):
                    total = jnp.zeros((32, 128), jnp.float32)
                    for kk in range(4):
                        total += straight[kk] * masks[dx * 2 + c, pl.ds(2 * kk, 1), :]
                        total += turned[kk] * masks[dx * 2 + c, pl.ds(2 * kk + 1, 1), :]
                    if c == 0:
                        one_own[dx, position] = total
                    else:
                        one_out[dx, position] = total.astype(jnp.bfloat16)
        stage_one(step).start()

    def middle(step):
        lo, hi = GROUPS[step]
        stage_one(step).wait_recv()
        for dx in range(NX):
            for position in range(lo, hi):
                total = one_own[dx, position] + one_in[dx, position].astype(jnp.float32)
                if dx == 0:
                    one_own[0, position] = total
                else:
                    two_out[dx - 1, position] = total.astype(jnp.bfloat16)
            if dx:
                stage_two(step, dx).start()

    def finish(step):
        lo, hi = GROUPS[step]
        for dx in range(1, NX):
            stage_two(step, dx).wait_recv()
        for position in range(lo, hi):
            total = one_own[0, position]
            for dx in range(1, NX):
                total += two_in[dx - 1, position].astype(jnp.float32)
            final[position] = total.reshape(NY, ROWS, 128).astype(jnp.bfloat16)
            for dy in range(NY):
                if ORDER[position] or dy:
                    deliver(position, dy).start()
                else:
                    landed[pair] = total[:ROWS].astype(jnp.bfloat16)

    plan = {
        1: [lambda: flip_block(0), lambda: flip_block(1), lambda: flip_block(2), lambda: flip_block(3)],
        2: [lambda n=n: compute((0, 1, -1), n) for n in range(4)],
        3: [lambda n=n: compute((2, -2), n) for n in range(4)],
        4: [lambda n=n: compute((3, -3), n) for n in range(4)],
        5: [lambda n=n: compute((4, -4), n) for n in range(4)] + [lambda: spread(4)],
        6: [lambda n=n: compute((5, -5), n) for n in range(4)] + [lambda: spread(5), lambda: middle(4)],
        7: [lambda n=n: compute((6, -6), n) for n in range(4)] + [lambda: spread(6), lambda: (middle(5), finish(4))],
        8: [lambda n=n: compute((7, -7), n) for n in range(4)] + [lambda: spread(7), lambda: (middle(6), finish(5))],
    }

    def forward_first():
        for way in (1, -1):
            y_a(way).wait_recv()
            y_a2(way).start()
            for to in (1, -1):
                z_a(1, to, -way % NY).start()
        for way in (1, -1):
            y_b(0, way).wait_recv()
            y_b2(0, way).start()
        for way in (1, -1):
            y_a2(way).wait_recv()
        for to in (1, -1):
            z_a(1, to, 2).start()

    forward_first()
    for s in range(1, 8):
        jobs = plan[s]

        def job(i):
            if i < len(jobs):
                jobs[i]()

        for way in (1, -1):
            z_b(s, way).wait_recv()
            z_b(s + 1, way).start()
            for to in (1, -1):
                y_b(-way * s, to).start()
        for i, dy in enumerate((0, 1, 3, 2)):
            for way in (1, -1):
                z_a(s, way, dy).wait_recv()
                if s + 1 < 8 or (dy < 2) == (way == 1):
                    z_a(s + 1, way, dy).start()
            if i == 1:
                if s > 1:
                    for dz in (1 - s, s - 1):
                        for way in (1, -1):
                            y_b2(dz, way).wait_recv()
                else:
                    for way in (1, -1):
                        y_b2(0, way).wait_recv()
                job(0)
            if i == 2:
                job(1)
        for dz in (-s, s):
            for way in (1, -1):
                y_b(dz, way).wait_recv()
                y_b2(dz, way).start()
        for i in range(2, len(jobs)):
            job(i)

    for way in (1, -1):
        z_b(8, way).wait_recv()
    for way in (1, -1):
        y_b(8, way).start()
    for dz in (-7, 7):
        for way in (1, -1):
            y_b2(dz, way).wait_recv()
    plan[8][0]()
    plan[8][1]()
    for way in (1, -1):
        y_b(8, way).wait_recv()
        y_b2(8, way).start()
    for one in plan[8][2:]:
        one()
    for dy in range(NY):
        z_a(8, 1 if dy < 2 else -1, dy).wait_recv()
    for way in (1, -1):
        y_b2(8, way).wait_recv()
    for n in range(4):
        compute((8,), n)
    spread(8)
    middle(7)
    finish(6)
    middle(8)
    finish(7)
    finish(8)

    for position in range(NZ):
        for dy in range(NY):
            if ORDER[position] or dy:
                deliver(position, dy).wait_recv()

    natural = jnp.zeros((ROWS, 1), jnp.int32)
    for r in range(ROWS):
        natural = jnp.where(rows_iota == r, place[r], natural)
    low = lax.broadcasted_iota(jnp.int32, (ROWS, 128), 1) < 64
    for m in range(32):
        blocks = []
        for j in (2 * m, 2 * m + 1):
            found = landed[j].astype(jnp.float32)
            picked = jnp.zeros((ROWS, 128), jnp.float32)
            for i in range(ROWS):
                picked = jnp.where(natural == i, found[i:i + 1, :], picked)
            blocks.append(picked)
        cols = pl.ds(128 * m, 128)
        out[0, :, cols] = jnp.where(low, blocks[0], pltpu.roll(blocks[1], 64, 1)).astype(jnp.bfloat16)
        out[1, :, cols] = jnp.where(low, pltpu.roll(blocks[0], 64, 1), blocks[1]).astype(jnp.bfloat16)

    for one in table.values():
        one.wait_send()


MESSAGES = 16 + 60 + 32 + 32 + 4 + 5 + 15 + 63


def shards(amplitudes, partner, integrals, pattern, owner):
    vmem = pl.BlockSpec(memory_space=pltpu.VMEM)
    smem = pl.BlockSpec(memory_space=pltpu.SMEM)
    result = pl.pallas_call(
        kernel,
        out_shape=jax.ShapeDtypeStruct((2, ROWS, TT), jnp.bfloat16),
        in_specs=[vmem, pl.BlockSpec(memory_space=pl.ANY), smem, smem, smem],
        out_specs=vmem,
        scratch_shapes=[
            pltpu.VMEM((NZ, NY, ROWS, TT), jnp.bfloat16),
            pltpu.VMEM((512, TT), jnp.bfloat16),
            pltpu.VMEM((64, 64, 512), jnp.bfloat16),
            pltpu.VMEM((NZ, 32, 512), jnp.float32),
            pltpu.VMEM((512, 512), jnp.bfloat16),
            pltpu.VMEM((8, 8, 128), jnp.float32),
            pltpu.VMEM((NX, NZ, 32, 128), jnp.bfloat16),
            pltpu.VMEM((NX, NZ, 32, 128), jnp.float32),
            pltpu.VMEM((NX, NZ, 32, 128), jnp.bfloat16),
            pltpu.VMEM((NX - 1, NZ, 32, 128), jnp.bfloat16),
            pltpu.VMEM((NX - 1, NZ, 32, 128), jnp.bfloat16),
            pltpu.VMEM((NZ, NY, ROWS, 128), jnp.bfloat16),
            pltpu.VMEM((NZ * NY, ROWS, 128), jnp.bfloat16),
            pltpu.SemaphoreType.DMA,
            pltpu.SemaphoreType.DMA((MESSAGES,)),
            pltpu.SemaphoreType.DMA((MESSAGES,)),
        ],
        compiler_params=pltpu.CompilerParams(collective_id=0, has_side_effects=True, vmem_limit_bytes=60 * 2**20),
    )(amplitudes.reshape(ROWS, TT), integrals.reshape(512, TT), partner, pattern, owner)
    return jnp.swapaxes(result, 0, 1)


def solution(mesh):
    return jax.shard_map(
        shards,
        mesh=mesh,
        in_specs=(P("pair", "virt", None), P("pair"), P("virt", "pair", None), P("virt"), P()),
        out_specs=P("pair", "virt", None),
        check_vma=False,
    )
```

```python
import jax
import jax.numpy as jnp
from jax import lax
from jax.experimental import pallas as pl
from jax.experimental.pallas import tpu as pltpu
from jax.sharding import PartitionSpec as P

MESH = pl.DeviceIdType.MESH
NZ, NY, NX = 16, 4, 4
NB = NZ // 2
ROWS = 8
TT = 4096
CUT = 1536
HALF = (TT - CUT) // 2
ORDER = (0, 1, 7, 2, 6, 3, 5, 4)
GROUPS = ((0, 1), (1, 3), (3, 5), (5, 7), (7, 8))

ACOLS = pl.ds(0, CUT)
BCOLS = pl.ds(CUT, TT - CUT)
BHALF = {1: pl.ds(CUT, HALF), -1: pl.ds(CUT + HALF, HALF)}


def kernel(amp, ints, partner, pattern, owner, out, mine, met, gath, tile, flip, acc, perm, masks,
           one_out, one_own, one_in, two_out, two_in, final, landed, load_sem, send, recv):
    pair = lax.axis_index("pair")
    virt = lax.axis_index("virt")
    z, y = pair // NY, pair % NY
    x, core = virt // 2, virt % 2

    def at(dz, dy):
        return ((z + (dz % NZ)) % NZ * NY + (y + (dy % NY)) % NY, virt)

    def beside(dx, swap):
        return (pair, (x + dx) % NX * 2 + (1 - core if swap else core))

    load = pltpu.make_async_copy(ints, tile, load_sem)
    load.start()

    table = {}

    def message(key, src, dst, device):
        if key not in table:
            slot = len(table)
            table[key] = pltpu.make_async_remote_copy(
                src_ref=src, dst_ref=dst, send_sem=send.at[slot], recv_sem=recv.at[slot],
                device_id=device, device_id_type=MESH)
        return table[key]

    def meet(part, way):
        cols = ACOLS if part == 0 else BCOLS
        return message(("meet", part, way), mine.at[:, cols], met.at[(1 - way) // 2, :, cols], at(4 * way, 0))

    def z_b(far, way):
        if far < 3:
            return message(("zb", far, way), gath.at[0, 0, :, BCOLS], gath.at[(-way * far) % NB, 0, :, BCOLS], at(way * far, 0))
        cols = BCOLS if far == 3 else BHALF[way]
        return message(("zb", far, way), gath.at[(-way * 2) % NB, 0, :, cols],
                       gath.at[(-way * far) % NB, 0, :, cols], at(way * (far - 2), 0))

    def z_a(s, way, dy):
        return message(("za", s, way, dy), gath.at[(-way * (s - 1)) % NB, dy, :, ACOLS],
                       gath.at[(-way * s) % NB, dy, :, ACOLS], at(way, 0))

    def y_b(dz, way):
        dz %= NB
        return message(("yb", dz, way), gath.at[dz, 0, :, BCOLS], gath.at[dz, -way % NY, :, BCOLS], at(0, way))

    def y_b2(dz, way):
        dz %= NB
        return message(("yb2", dz, way), gath.at[dz, -way % NY, :, BHALF[way]], gath.at[dz, 2, :, BHALF[way]], at(0, way))

    def y_a(way):
        return message(("ya", way), gath.at[0, 0, :, ACOLS], gath.at[0, -way % NY, :, ACOLS], at(0, way))

    def stage_one(group):
        lo, hi = GROUPS[group]
        return message(("one", group), one_out.at[:, 2 * lo:2 * hi], one_in.at[:, 2 * lo:2 * hi], beside(0, True))

    def stage_two(group, dx):
        lo, hi = GROUPS[group]
        return message(("two", group, dx), two_out.at[dx - 1, 2 * lo:2 * hi], two_in.at[dx - 1, 2 * lo:2 * hi], beside(dx, False))

    def upper(dz):
        return (z + (dz % NZ)) % NZ // NB

    def deliver(index, side, dy):
        dz = ORDER[index] + 4 * side
        return message(("out", index, side, dy), final.at[2 * index + upper(dz), dy], landed.at[pair], at(dz, dy))

    rows_iota = lax.broadcasted_iota(jnp.int32, (ROWS, 1), 0)
    lower = z < NB
    place = [jnp.where(lower, r, partner[r] % ROWS) for r in range(ROWS)]
    plain = amp[...].astype(jnp.float32)
    sorted_rows = jnp.zeros((ROWS, TT), jnp.float32)
    for r in range(ROWS):
        sorted_rows = jnp.where(rows_iota == place[r], plain[r:r + 1, :], sorted_rows)
    mine[...] = sorted_rows.astype(jnp.bfloat16)

    barrier = pltpu.get_barrier_semaphore()
    friends = [at(4, 0), at(-4, 0), at(1, 0), at(-1, 0), at(2, 0), at(-2, 0), at(0, 1), at(0, -1), at(0, 2),
               beside(0, True), beside(1, False), beside(2, False), beside(3, False)]
    for friend in friends:
        pl.semaphore_signal(barrier, inc=1, device_id=friend, device_id_type=MESH)

    lanes = lax.broadcasted_iota(jnp.int32, (1, 128), 1)
    for dx in range(NX):
        for c in range(2):
            to = (x + dx) % NX * 2 + (core if c == 0 else 1 - core)
            first, second = owner[2 * to], owner[2 * to + 1]
            for kk in range(4):
                even, odd = pattern[2 * kk], pattern[2 * kk + 1]

                def hit(tile_id, slot_id):
                    return jnp.where(tile_id == slot_id, jnp.float32(1), jnp.float32(0))

                masks[dx * 2 + c, pl.ds(2 * kk, 1), :] = jnp.where(lanes < 64, hit(even, first), hit(odd, second))
                masks[dx * 2 + c, pl.ds(2 * kk + 1, 1), :] = jnp.where(lanes < 64, hit(odd, first), hit(even, second))

    pl.semaphore_wait(barrier, len(friends))
    for part in range(2):
        for way in (1, -1):
            meet(part, way).start()

    row = lax.broadcasted_iota(jnp.int32, (512, 512), 0)
    col = lax.broadcasted_iota(jnp.int32, (512, 512), 1)
    perm[...] = jnp.where(col == (row % 8) * 64 + row // 8, 1.0, 0.0).astype(jnp.bfloat16)
    load.wait()

    def flip_block(i):
        parts = []
        for h in range(2):
            cols = pl.ds(i * 1024 + h * 512, 512)
            turned = lax.dot_general(perm[...], tile[:, cols], (((1,), (1,)), ((), ())), preferred_element_type=jnp.float32)
            parts.append(turned.reshape(64, 8, 512))
        flip[:, pl.ds(i * 16, 16), :] = jnp.concatenate(parts, axis=1).astype(jnp.bfloat16)

    def compute(group, n):
        lo, hi = GROUPS[group]
        blocks = ORDER[lo:hi]
        left = jnp.concatenate([gath[dz].reshape(NY * ROWS, TT) for dz in blocks], axis=0)
        if n < 2:
            right = tile[pl.ds(n * 256, 256), :]
            got = lax.dot_general(left, right, (((1,), (1,)), ((), ())), preferred_element_type=jnp.float32)
        else:
            right = flip[:, :, pl.ds((n - 2) * 256, 256)].reshape(TT, 256)
            got = jnp.dot(left, right, preferred_element_type=jnp.float32)
        for i in range(len(blocks)):
            acc[2 * (lo + i) + n // 2, :, pl.ds(n % 2 * 256, 256)] = got[i * 32:(i + 1) * 32]

    def spread(group):
        lo, hi = GROUPS[group]
        for position in range(2 * lo, 2 * hi):
            straight = [acc[position, :, pl.ds(128 * kk, 128)] for kk in range(4)]
            turned = [pltpu.roll(v, 64, 1) for v in straight]
            for dx in range(NX):
                for c in range(2):
                    total = jnp.zeros((32, 128), jnp.float32)
                    for kk in range(4):
                        total += straight[kk] * masks[dx * 2 + c, pl.ds(2 * kk, 1), :]
                        total += turned[kk] * masks[dx * 2 + c, pl.ds(2 * kk + 1, 1), :]
                    if c == 0:
                        one_own[dx, position] = total
                    else:
                        one_out[dx, position] = total.astype(jnp.bfloat16)
        stage_one(group).start()

    def middle(group):
        lo, hi = GROUPS[group]
        stage_one(group).wait_recv()
        for dx in (1, 2, 3, 0):
            for position in range(2 * lo, 2 * hi):
                total = one_own[dx, position] + one_in[dx, position].astype(jnp.float32)
                if dx == 0:
                    one_own[0, position] = total
                else:
                    two_out[dx - 1, position] = total.astype(jnp.bfloat16)
            if dx:
                stage_two(group, dx).start()

    def finish(group):
        lo, hi = GROUPS[group]
        for dx in range(1, NX):
            stage_two(group, dx).wait_recv()
        for position in range(2 * lo, 2 * hi):
            total = one_own[0, position]
            for dx in range(1, NX):
                total += two_in[dx - 1, position].astype(jnp.float32)
            final[position] = total.reshape(NY, ROWS, 128).astype(jnp.bfloat16)
        for index in range(lo, hi):
            for side in (1, -1):
                for dy in (2, 1, 3, 0):
                    if (ORDER[index] + 4 * side) % NZ or dy:
                        deliver(index, side, dy).start()
                    else:
                        landed[pair] = final[2 * index + upper(0), 0]

    def add_up(cols):
        gath[0, 0, :, cols] = (met[0, :, cols].astype(jnp.float32) + met[1, :, cols].astype(jnp.float32)).astype(jnp.bfloat16)

    def pass_b(*blocks):
        for dz in blocks:
            for way in (1, -1):
                y_b(dz, way).start()

    def relay_b(*blocks):
        for dz in blocks:
            for way in (1, -1):
                y_b(dz, way).wait_recv()
                y_b2(dz, way).start()

    def whole_b(*blocks):
        for dz in blocks:
            for way in (1, -1):
                y_b2(dz, way).wait_recv()

    def ways(s, dy):
        return (1, -1) if s < 4 else ((1,) if dy < 2 else (-1,))

    def relay_a(s):
        for dy in (0, 1, 3, 2):
            for way in ways(s, dy):
                z_a(s, way, dy).wait_recv()
                if s < 4 and way in ways(s + 1, dy):
                    z_a(s + 1, way, dy).start()

    for i in range(3):
        flip_block(i)

    for way in (1, -1):
        meet(0, way).wait_recv()
    add_up(ACOLS)
    for way in (1, -1, 2):
        y_a(way).start()
    for way in (1, -1):
        meet(1, way).wait_recv()
    add_up(BCOLS)
    for way in (1, -1):
        z_b(2, way).start()
        z_b(1, way).start()
    for way in (1, -1):
        z_a(1, way, 0).start()
    pass_b(0)
    for way in (1, -1, 2):
        y_a(way).wait_recv()
        for to in (1, -1):
            z_a(1, to, -way % NY).start()

    flip_block(3)
    for way in (1, -1):
        z_b(1, way).wait_recv()
    pass_b(1, -1)
    for way in (1, -1):
        z_b(2, way).wait_recv()
        z_b(4, way).start()
        z_b(3, way).start()
    relay_b(0)
    pass_b(2, -2)
    relay_a(1)
    whole_b(0)
    compute(0, 0)
    compute(0, 1)
    relay_b(1, -1)
    compute(0, 2)
    compute(0, 3)
    for way in (1, -1):
        z_b(4, way).wait_recv()
        z_b(3, way).wait_recv()
    pass_b(4, 3, -3)
    relay_a(2)
    relay_b(2, -2)
    spread(0)
    whole_b(1, -1)
    compute(1, 0)
    compute(1, 1)
    relay_b(4, 3, -3)
    relay_a(3)
    compute(1, 2)
    compute(1, 3)
    spread(1)
    middle(0)
    whole_b(2, -2)
    for n in range(4):
        compute(2, n)
    spread(2)
    middle(1)
    finish(0)
    whole_b(3, -3)
    for n in range(4):
        compute(3, n)
    spread(3)
    middle(2)
    finish(1)
    relay_a(4)
    whole_b(4)
    for n in range(4):
        compute(4, n)
    spread(4)
    middle(3)
    finish(2)
    middle(4)
    finish(3)
    finish(4)

    for index in range(NB):
        for side in (1, -1):
            for dy in range(NY):
                if (ORDER[index] + 4 * side) % NZ or dy:
                    deliver(index, side, dy).wait_recv()

    natural = jnp.zeros((ROWS, 1), jnp.int32)
    for r in range(ROWS):
        natural = jnp.where(rows_iota == r, place[r], natural)
    low = lax.broadcasted_iota(jnp.int32, (ROWS, 128), 1) < 64
    for m in range(32):
        blocks = []
        for j in (2 * m, 2 * m + 1):
            found = landed[j].astype(jnp.float32)
            picked = jnp.zeros((ROWS, 128), jnp.float32)
            for i in range(ROWS):
                picked = jnp.where(natural == i, found[i:i + 1, :], picked)
            blocks.append(picked)
        cols = pl.ds(128 * m, 128)
        out[0, :, cols] = jnp.where(low, blocks[0], pltpu.roll(blocks[1], 64, 1)).astype(jnp.bfloat16)
        out[1, :, cols] = jnp.where(low, pltpu.roll(blocks[0], 64, 1), blocks[1]).astype(jnp.bfloat16)

    for one in table.values():
        one.wait_send()


MESSAGES = 4 + 8 + 28 + 16 + 16 + 3 + 5 + 15 + 63


def shards(amplitudes, partner, integrals, pattern, owner):
    plain = amplitudes.reshape(ROWS, TT)
    turned = jnp.swapaxes(plain.reshape(ROWS, 64, 64), 1, 2).reshape(ROWS, TT)
    plain = jnp.where(lax.axis_index("pair") < NB * NY, plain, turned)
    vmem = pl.BlockSpec(memory_space=pltpu.VMEM)
    smem = pl.BlockSpec(memory_space=pltpu.SMEM)
    result = pl.pallas_call(
        kernel,
        out_shape=jax.ShapeDtypeStruct((2, ROWS, TT), jnp.bfloat16),
        in_specs=[vmem, pl.BlockSpec(memory_space=pl.ANY), smem, smem, smem],
        out_specs=vmem,
        scratch_shapes=[
            pltpu.VMEM((ROWS, TT), jnp.bfloat16),
            pltpu.VMEM((2, ROWS, TT), jnp.bfloat16),
            pltpu.VMEM((NB, NY, ROWS, TT), jnp.bfloat16),
            pltpu.VMEM((512, TT), jnp.bfloat16),
            pltpu.VMEM((64, 64, 512), jnp.bfloat16),
            pltpu.VMEM((NZ, 32, 512), jnp.float32),
            pltpu.VMEM((512, 512), jnp.bfloat16),
            pltpu.VMEM((8, 8, 128), jnp.float32),
            pltpu.VMEM((NX, NZ, 32, 128), jnp.bfloat16),
            pltpu.VMEM((NX, NZ, 32, 128), jnp.float32),
            pltpu.VMEM((NX, NZ, 32, 128), jnp.bfloat16),
            pltpu.VMEM((NX - 1, NZ, 32, 128), jnp.bfloat16),
            pltpu.VMEM((NX - 1, NZ, 32, 128), jnp.bfloat16),
            pltpu.VMEM((NZ, NY, ROWS, 128), jnp.bfloat16),
            pltpu.VMEM((NZ * NY, ROWS, 128), jnp.bfloat16),
            pltpu.SemaphoreType.DMA,
            pltpu.SemaphoreType.DMA((MESSAGES,)),
            pltpu.SemaphoreType.DMA((MESSAGES,)),
        ],
        compiler_params=pltpu.CompilerParams(collective_id=0, has_side_effects=True, vmem_limit_bytes=60 * 2**20),
    )(plain, integrals.reshape(512, TT), partner, pattern, owner)
    return jnp.swapaxes(result, 0, 1)


def solution(mesh):
    return jax.shard_map(
        shards,
        mesh=mesh,
        in_specs=(P("pair", "virt", None), P("pair"), P("virt", "pair", None), P("virt"), P()),
        out_specs=P("pair", "virt", None),
        check_vma=False,
    )
```

```python
import jax
import jax.numpy as jnp
from jax import lax
from jax.experimental import pallas as pl
from jax.experimental.pallas import tpu as pltpu
from jax.sharding import PartitionSpec as P

MESH = pl.DeviceIdType.MESH
NZ, NY, NX = 16, 4, 4
NB = NZ // 2
ROWS = 8
TT = 4096
CUT = 1536
HALF = (TT - CUT) // 2
ORDER = (0, 1, 7, 2, 6, 3, 5, 4)
GROUPS = ((0, 1), (1, 3), (3, 5), (5, 8))

ACOLS = pl.ds(0, CUT)
BCOLS = pl.ds(CUT, TT - CUT)
BHALF = {1: pl.ds(CUT, HALF), -1: pl.ds(CUT + HALF, HALF)}


def kernel(amp, ints, partner, pattern, owner, out, mine, met, gath, tile, flip, acc, perm, masks,
           one_out, one_own, one_in, two_out, two_in, final, landed, load_sem, send, recv):
    pair = lax.axis_index("pair")
    virt = lax.axis_index("virt")
    z, y = pair // NY, pair % NY
    x, core = virt // 2, virt % 2

    def at(dz, dy):
        return ((z + (dz % NZ)) % NZ * NY + (y + (dy % NY)) % NY, virt)

    def beside(dx, swap):
        return (pair, (x + dx) % NX * 2 + (1 - core if swap else core))

    load = pltpu.make_async_copy(ints, tile, load_sem)
    load.start()

    table = {}

    def message(key, src, dst, device):
        if key not in table:
            slot = len(table)
            table[key] = pltpu.make_async_remote_copy(
                src_ref=src, dst_ref=dst, send_sem=send.at[slot], recv_sem=recv.at[slot],
                device_id=device, device_id_type=MESH)
        return table[key]

    def meet(part, way):
        cols = ACOLS if part == 0 else BCOLS
        return message(("meet", part, way), mine.at[:, cols], met.at[(1 - way) // 2, :, cols], at(4 * way, 0))

    def z_b(far, way):
        if far < 3:
            return message(("zb", far, way), gath.at[0, 0, :, BCOLS], gath.at[(-way * far) % NB, 0, :, BCOLS], at(way * far, 0))
        cols = BCOLS if far == 3 else BHALF[way]
        return message(("zb", far, way), gath.at[(-way * 2) % NB, 0, :, cols],
                       gath.at[(-way * far) % NB, 0, :, cols], at(way * (far - 2), 0))

    def z_a(far, way, dy):
        origin = 0 if far < 3 else (-way * 2) % NB
        return message(("za", far, way, dy), gath.at[origin, dy, :, ACOLS],
                       gath.at[(-way * far) % NB, dy, :, ACOLS], at(way * (far if far < 3 else far - 2), 0))

    def y_b(dz, way):
        dz %= NB
        return message(("yb", dz, way), gath.at[dz, 0, :, BCOLS], gath.at[dz, -way % NY, :, BCOLS], at(0, way))

    def y_b2(dz, way):
        dz %= NB
        return message(("yb2", dz, way), gath.at[dz, -way % NY, :, BHALF[way]], gath.at[dz, 2, :, BHALF[way]], at(0, way))

    def y_a(way):
        return message(("ya", way), gath.at[0, 0, :, ACOLS], gath.at[0, -way % NY, :, ACOLS], at(0, way))

    def stage_one(group):
        lo, hi = GROUPS[group]
        return message(("one", group), one_out.at[:, 2 * lo:2 * hi], one_in.at[:, 2 * lo:2 * hi], beside(0, True))

    def stage_two(group, dx):
        lo, hi = GROUPS[group]
        return message(("two", group, dx), two_out.at[dx - 1, 2 * lo:2 * hi], two_in.at[dx - 1, 2 * lo:2 * hi], beside(dx, False))

    def upper(dz):
        return (z + (dz % NZ)) % NZ // NB

    def deliver(index, side, dy):
        dz = ORDER[index] + 4 * side
        return message(("out", index, side, dy), final.at[2 * index + upper(dz), dy], landed.at[pair], at(dz, dy))

    barrier = pltpu.get_barrier_semaphore()
    friends = [at(4, 0), at(-4, 0), at(1, 0), at(-1, 0), at(2, 0), at(-2, 0), at(0, 1), at(0, -1), at(0, 2),
               beside(0, True), beside(1, False), beside(2, False), beside(3, False)]
    for friend in friends:
        pl.semaphore_signal(barrier, inc=1, device_id=friend, device_id_type=MESH)

    row = lax.broadcasted_iota(jnp.int32, (512, 512), 0)
    col = lax.broadcasted_iota(jnp.int32, (512, 512), 1)
    perm[...] = jnp.where(col == (row % 8) * 64 + row // 8, 1.0, 0.0).astype(jnp.bfloat16)
    rows_iota = lax.broadcasted_iota(jnp.int32, (ROWS, 1), 0)
    lower = z < NB
    place = [jnp.where(lower, r, partner[r] % ROWS) for r in range(ROWS)]
    plain = amp[...].astype(jnp.float32)
    sorted_rows = jnp.zeros((ROWS, TT), jnp.float32)
    for r in range(ROWS):
        sorted_rows = jnp.where(rows_iota == place[r], plain[r:r + 1, :], sorted_rows)

    def exchange(value, order):
        return lax.dot_general(value.astype(jnp.bfloat16), order, (((1,), (1,)), ((), ())), preferred_element_type=jnp.float32)

    low = lax.broadcasted_iota(jnp.int32, (ROWS, 128), 1) < 64
    stacked = jnp.concatenate([sorted_rows[:, 512 * b:512 * (b + 1)] for b in range(8)], axis=0)
    once = exchange(stacked, perm[...])
    regrouped = []
    for e in range(8):
        pieces = []
        for k in range(4):
            first = once[16 * k:16 * k + 8, 128 * (e // 2):128 * (e // 2 + 1)]
            second = once[16 * k + 8:16 * k + 16, 128 * (e // 2):128 * (e // 2 + 1)]
            if e % 2:
                pieces.append(jnp.where(low, pltpu.roll(first, 64, 1), second))
            else:
                pieces.append(jnp.where(low, first, pltpu.roll(second, 64, 1)))
        regrouped.append(jnp.concatenate(pieces, axis=1))
    second_order = jnp.where(col == row % 64 // 8 * 64 + row // 64 * 8 + row % 8, 1.0, 0.0).astype(jnp.bfloat16)
    twice = exchange(jnp.concatenate(regrouped, axis=0), second_order)
    for e in range(8):
        cols = pl.ds(512 * e, 512)
        mine[:, cols] = jnp.where(lower, sorted_rows[:, 512 * e:512 * (e + 1)], twice[8 * e:8 * (e + 1)]).astype(jnp.bfloat16)


    lanes = lax.broadcasted_iota(jnp.int32, (1, 128), 1)
    for dx in range(NX):
        for c in range(2):
            to = (x + dx) % NX * 2 + (core if c == 0 else 1 - core)
            first, second = owner[2 * to], owner[2 * to + 1]
            for kk in range(4):
                even, odd = pattern[2 * kk], pattern[2 * kk + 1]

                def hit(tile_id, slot_id):
                    return jnp.where(tile_id == slot_id, jnp.float32(1), jnp.float32(0))

                masks[dx * 2 + c, pl.ds(2 * kk, 1), :] = jnp.where(lanes < 64, hit(even, first), hit(odd, second))
                masks[dx * 2 + c, pl.ds(2 * kk + 1, 1), :] = jnp.where(lanes < 64, hit(odd, first), hit(even, second))

    pl.semaphore_wait(barrier, len(friends))
    for part in range(2):
        for way in (1, -1):
            meet(part, way).start()

    load.wait()

    def flip_block(i):
        parts = []
        for h in range(2):
            cols = pl.ds(i * 1024 + h * 512, 512)
            turned = lax.dot_general(perm[...], tile[:, cols], (((1,), (1,)), ((), ())), preferred_element_type=jnp.float32)
            parts.append(turned.reshape(64, 8, 512))
        flip[:, pl.ds(i * 16, 16), :] = jnp.concatenate(parts, axis=1).astype(jnp.bfloat16)

    def compute(group, n):
        lo, hi = GROUPS[group]
        blocks = ORDER[lo:hi]
        left = jnp.concatenate([gath[dz].reshape(NY * ROWS, TT) for dz in blocks], axis=0)
        if n < 2:
            right = tile[pl.ds(n * 256, 256), :]
            got = lax.dot_general(left, right, (((1,), (1,)), ((), ())), preferred_element_type=jnp.float32)
        else:
            right = flip[:, :, pl.ds((n - 2) * 256, 256)].reshape(TT, 256)
            got = jnp.dot(left, right, preferred_element_type=jnp.float32)
        for i in range(len(blocks)):
            acc[2 * (lo + i) + n // 2, :, pl.ds(n % 2 * 256, 256)] = got[i * 32:(i + 1) * 32]

    def spread(group):
        lo, hi = GROUPS[group]
        for position in range(2 * lo, 2 * hi):
            straight = [acc[position, :, pl.ds(128 * kk, 128)] for kk in range(4)]
            turned = [pltpu.roll(v, 64, 1) for v in straight]
            for dx in range(NX):
                for c in range(2):
                    total = jnp.zeros((32, 128), jnp.float32)
                    for kk in range(4):
                        total += straight[kk] * masks[dx * 2 + c, pl.ds(2 * kk, 1), :]
                        total += turned[kk] * masks[dx * 2 + c, pl.ds(2 * kk + 1, 1), :]
                    if c == 0:
                        one_own[dx, position] = total
                    else:
                        one_out[dx, position] = total.astype(jnp.bfloat16)
        stage_one(group).start()

    def middle(group):
        lo, hi = GROUPS[group]
        stage_one(group).wait_recv()
        for dx in (1, 2, 3, 0):
            for position in range(2 * lo, 2 * hi):
                total = one_own[dx, position] + one_in[dx, position].astype(jnp.float32)
                if dx == 0:
                    one_own[0, position] = total
                else:
                    two_out[dx - 1, position] = total.astype(jnp.bfloat16)
            if dx:
                stage_two(group, dx).start()

    def finish(group):
        lo, hi = GROUPS[group]
        for dx in range(1, NX):
            stage_two(group, dx).wait_recv()
        for position in range(2 * lo, 2 * hi):
            total = one_own[0, position]
            for dx in range(1, NX):
                total += two_in[dx - 1, position].astype(jnp.float32)
            final[position] = total.reshape(NY, ROWS, 128).astype(jnp.bfloat16)
        for index in range(lo, hi):
            for side in (1, -1):
                for dy in (2, 1, 3, 0):
                    if (ORDER[index] + 4 * side) % NZ or dy:
                        deliver(index, side, dy).start()
                    else:
                        landed[pair] = final[2 * index + upper(0), 0]

    def add_up(cols):
        gath[0, 0, :, cols] = (met[0, :, cols].astype(jnp.float32) + met[1, :, cols].astype(jnp.float32)).astype(jnp.bfloat16)

    def pass_b(*blocks):
        for dz in blocks:
            for way in (1, -1):
                y_b(dz, way).start()

    def relay_b(*blocks):
        for dz in blocks:
            for way in (1, -1):
                y_b(dz, way).wait_recv()
                y_b2(dz, way).start()

    def whole_b(*blocks):
        for dz in blocks:
            for way in (1, -1):
                y_b2(dz, way).wait_recv()

    def ends_a(dy):
        return 1 if dy < 2 else -1

    def send_a(dy):
        for far in (2, 1):
            for way in (1, -1):
                z_a(far, way, dy).start()

    def relay_a(*dys):
        for dy in dys:
            for way in (1, -1):
                z_a(2, way, dy).wait_recv()
                if way == ends_a(dy):
                    z_a(4, way, dy).start()
                z_a(3, way, dy).start()

    def whole_a(far):
        for dy in range(NY):
            for way in (1, -1) if far < 4 else (ends_a(dy),):
                z_a(far, way, dy).wait_recv()

    for i in range(3):
        flip_block(i)

    for way in (1, -1):
        meet(0, way).wait_recv()
    add_up(ACOLS)
    for way in (1, -1, 2):
        y_a(way).start()
    send_a(0)
    for way in (1, -1):
        meet(1, way).wait_recv()
    add_up(BCOLS)
    for way in (1, -1):
        z_b(2, way).start()
        z_b(1, way).start()
    pass_b(0)
    for way in (1, -1, 2):
        y_a(way).wait_recv()
        send_a(-way % NY)

    flip_block(3)
    for way in (1, -1):
        z_b(1, way).wait_recv()
    pass_b(1, -1)
    relay_a(0)
    for way in (1, -1):
        z_b(2, way).wait_recv()
        z_b(4, way).start()
        z_b(3, way).start()
    relay_b(0)
    pass_b(2, -2)
    relay_a(3, 1, 2)
    whole_b(0)
    compute(0, 0)
    compute(0, 1)
    relay_b(1, -1)
    for way in (1, -1):
        z_b(4, way).wait_recv()
        z_b(3, way).wait_recv()
    pass_b(4, 3, -3)
    compute(0, 2)
    compute(0, 3)
    relay_b(2, -2)
    spread(0)
    whole_a(1)
    whole_b(1, -1)
    compute(1, 0)
    compute(1, 1)
    relay_b(4, 3, -3)
    compute(1, 2)
    compute(1, 3)
    spread(1)
    middle(0)
    whole_b(2, -2)
    for n in range(4):
        compute(2, n)
    spread(2)
    middle(1)
    finish(0)
    whole_a(3)
    whole_a(4)
    whole_b(4, 3, -3)
    for n in range(4):
        compute(3, n)
    spread(3)
    middle(2)
    finish(1)
    middle(3)
    finish(2)
    finish(3)

    for index in range(NB):
        for side in (1, -1):
            for dy in range(NY):
                if (ORDER[index] + 4 * side) % NZ or dy:
                    deliver(index, side, dy).wait_recv()

    natural = jnp.zeros((ROWS, 1), jnp.int32)
    for r in range(ROWS):
        natural = jnp.where(rows_iota == r, place[r], natural)
    for m in range(32):
        blocks = []
        for j in (2 * m, 2 * m + 1):
            found = landed[j].astype(jnp.float32)
            picked = jnp.zeros((ROWS, 128), jnp.float32)
            for i in range(ROWS):
                picked = jnp.where(natural == i, found[i:i + 1, :], picked)
            blocks.append(picked)
        cols = pl.ds(128 * m, 128)
        out[0, :, cols] = jnp.where(low, blocks[0], pltpu.roll(blocks[1], 64, 1)).astype(jnp.bfloat16)
        out[1, :, cols] = jnp.where(low, pltpu.roll(blocks[0], 64, 1), blocks[1]).astype(jnp.bfloat16)

    for one in table.values():
        one.wait_send()


MESSAGES = 4 + 8 + 28 + 16 + 16 + 3 + 4 + 12 + 63


def shards(amplitudes, partner, integrals, pattern, owner):
    plain = amplitudes.reshape(ROWS, TT)
    vmem = pl.BlockSpec(memory_space=pltpu.VMEM)
    smem = pl.BlockSpec(memory_space=pltpu.SMEM)
    result = pl.pallas_call(
        kernel,
        out_shape=jax.ShapeDtypeStruct((2, ROWS, TT), jnp.bfloat16),
        in_specs=[vmem, pl.BlockSpec(memory_space=pl.ANY), smem, smem, smem],
        out_specs=vmem,
        scratch_shapes=[
            pltpu.VMEM((ROWS, TT), jnp.bfloat16),
            pltpu.VMEM((2, ROWS, TT), jnp.bfloat16),
            pltpu.VMEM((NB, NY, ROWS, TT), jnp.bfloat16),
            pltpu.VMEM((512, TT), jnp.bfloat16),
            pltpu.VMEM((64, 64, 512), jnp.bfloat16),
            pltpu.VMEM((NZ, 32, 512), jnp.float32),
            pltpu.VMEM((512, 512), jnp.bfloat16),
            pltpu.VMEM((8, 8, 128), jnp.float32),
            pltpu.VMEM((NX, NZ, 32, 128), jnp.bfloat16),
            pltpu.VMEM((NX, NZ, 32, 128), jnp.float32),
            pltpu.VMEM((NX, NZ, 32, 128), jnp.bfloat16),
            pltpu.VMEM((NX - 1, NZ, 32, 128), jnp.bfloat16),
            pltpu.VMEM((NX - 1, NZ, 32, 128), jnp.bfloat16),
            pltpu.VMEM((NZ, NY, ROWS, 128), jnp.bfloat16),
            pltpu.VMEM((NZ * NY, ROWS, 128), jnp.bfloat16),
            pltpu.SemaphoreType.DMA,
            pltpu.SemaphoreType.DMA((MESSAGES,)),
            pltpu.SemaphoreType.DMA((MESSAGES,)),
        ],
        compiler_params=pltpu.CompilerParams(collective_id=0, has_side_effects=True, vmem_limit_bytes=60 * 2**20),
    )(plain, integrals.reshape(512, TT), partner, pattern, owner)
    return jnp.swapaxes(result, 0, 1)


def solution(mesh):
    return jax.shard_map(
        shards,
        mesh=mesh,
        in_specs=(P("pair", "virt", None), P("pair"), P("virt", "pair", None), P("virt"), P()),
        out_specs=P("pair", "virt", None),
        check_vma=False,
    )
```

```python
import jax
import jax.numpy as jnp
from jax import lax
from jax.experimental import pallas as pl
from jax.experimental.pallas import tpu as pltpu
from jax.sharding import PartitionSpec as P

MESH = pl.DeviceIdType.MESH
NZ, NY, NX = 16, 4, 4
NB = NZ // 2
ROWS = 8
TT = 4096
CUT = 1536
HALF = (TT - CUT) // 2
ORDER = (0, 1, 7, 2, 6, 3, 5, 4)
GROUPS = ((0, 1), (1, 3), (3, 5), (5, 8))

ACOLS = pl.ds(0, CUT)
BCOLS = pl.ds(CUT, TT - CUT)
BHALF = {1: pl.ds(CUT, HALF), -1: pl.ds(CUT + HALF, HALF)}


def kernel(amp, ints, partner, pattern, owner, out, mine, met, gath, tile, flip, acc, perm, masks,
           one_out, one_own, one_in, two_out, two_in, final, landed, load_sem, send, recv):
    pair = lax.axis_index("pair")
    virt = lax.axis_index("virt")
    z, y = pair // NY, pair % NY
    x, core = virt // 2, virt % 2

    def at(dz, dy):
        return ((z + (dz % NZ)) % NZ * NY + (y + (dy % NY)) % NY, virt)

    def beside(dx, swap):
        return (pair, (x + dx) % NX * 2 + (1 - core if swap else core))

    load = pltpu.make_async_copy(ints, tile, load_sem)
    load.start()

    table = {}

    def message(key, src, dst, device):
        if key not in table:
            slot = len(table)
            table[key] = pltpu.make_async_remote_copy(
                src_ref=src, dst_ref=dst, send_sem=send.at[slot], recv_sem=recv.at[slot],
                device_id=device, device_id_type=MESH)
        return table[key]

    def meet(part, way):
        cols = ACOLS if part == 0 else BCOLS
        return message(("meet", part, way), mine.at[:, cols], met.at[(1 - way) // 2, :, cols], at(4 * way, 0))

    def z_b(far, way):
        if far < 3:
            return message(("zb", far, way), gath.at[0, 0, :, BCOLS], gath.at[(-way * far) % NB, 0, :, BCOLS], at(way * far, 0))
        cols = BCOLS if far == 3 else BHALF[way]
        return message(("zb", far, way), gath.at[(-way * 2) % NB, 0, :, cols],
                       gath.at[(-way * far) % NB, 0, :, cols], at(way * (far - 2), 0))

    def z_a(far, way, dy):
        origin = 0 if far < 3 else (-way * 2) % NB
        return message(("za", far, way, dy), gath.at[origin, dy, :, ACOLS],
                       gath.at[(-way * far) % NB, dy, :, ACOLS], at(way * (far if far < 3 else far - 2), 0))

    def y_b(dz, way):
        dz %= NB
        return message(("yb", dz, way), gath.at[dz, 0, :, BCOLS], gath.at[dz, -way % NY, :, BCOLS], at(0, way))

    def y_b2(dz, way):
        dz %= NB
        return message(("yb2", dz, way), gath.at[dz, -way % NY, :, BHALF[way]], gath.at[dz, 2, :, BHALF[way]], at(0, way))

    def y_a(way):
        return message(("ya", way), gath.at[0, 0, :, ACOLS], gath.at[0, -way % NY, :, ACOLS], at(0, way))

    def stage_one(group):
        lo, hi = GROUPS[group]
        return message(("one", group), one_out.at[:, 2 * lo:2 * hi], one_in.at[:, 2 * lo:2 * hi], beside(0, True))

    def stage_two(group, dx):
        lo, hi = GROUPS[group]
        return message(("two", group, dx), two_out.at[dx - 1, 2 * lo:2 * hi], two_in.at[dx - 1, 2 * lo:2 * hi], beside(dx, False))

    def upper(dz):
        return (z + (dz % NZ)) % NZ // NB

    def deliver(index, side, dy):
        dz = ORDER[index] + 4 * side
        return message(("out", index, side, dy), final.at[2 * index + upper(dz), dy], landed.at[pair], at(dz, dy))

    barrier = pltpu.get_barrier_semaphore()
    friends = [at(4, 0), at(-4, 0), at(1, 0), at(-1, 0), at(2, 0), at(-2, 0), at(0, 1), at(0, -1), at(0, 2),
               beside(0, True), beside(1, False), beside(2, False), beside(3, False)]
    for friend in friends:
        pl.semaphore_signal(barrier, inc=1, device_id=friend, device_id_type=MESH)

    row = lax.broadcasted_iota(jnp.int32, (512, 512), 0)
    col = lax.broadcasted_iota(jnp.int32, (512, 512), 1)
    perm[...] = jnp.where(col == (row % 8) * 64 + row // 8, 1.0, 0.0).astype(jnp.bfloat16)
    rows_iota = lax.broadcasted_iota(jnp.int32, (ROWS, 1), 0)
    lower = z < NB
    place = [jnp.where(lower, r, partner[r] % ROWS) for r in range(ROWS)]
    plain = amp[...].astype(jnp.float32)
    sorted_rows = jnp.zeros((ROWS, TT), jnp.float32)
    for r in range(ROWS):
        sorted_rows = jnp.where(rows_iota == place[r], plain[r:r + 1, :], sorted_rows)

    def exchange(value, order):
        return lax.dot_general(value.astype(jnp.bfloat16), order, (((1,), (1,)), ((), ())), preferred_element_type=jnp.float32)

    low = lax.broadcasted_iota(jnp.int32, (ROWS, 128), 1) < 64
    stacked = jnp.concatenate([sorted_rows[:, 512 * b:512 * (b + 1)] for b in range(8)], axis=0)
    once = exchange(stacked, perm[...])
    regrouped = []
    for e in range(8):
        pieces = []
        for k in range(4):
            first = once[16 * k:16 * k + 8, 128 * (e // 2):128 * (e // 2 + 1)]
            second = once[16 * k + 8:16 * k + 16, 128 * (e // 2):128 * (e // 2 + 1)]
            if e % 2:
                pieces.append(jnp.where(low, pltpu.roll(first, 64, 1), second))
            else:
                pieces.append(jnp.where(low, first, pltpu.roll(second, 64, 1)))
        regrouped.append(jnp.concatenate(pieces, axis=1))
    second_order = jnp.where(col == row % 64 // 8 * 64 + row // 64 * 8 + row % 8, 1.0, 0.0).astype(jnp.bfloat16)
    twice = exchange(jnp.concatenate(regrouped, axis=0), second_order)
    for e in range(8):
        cols = pl.ds(512 * e, 512)
        mine[:, cols] = jnp.where(lower, sorted_rows[:, 512 * e:512 * (e + 1)], twice[8 * e:8 * (e + 1)]).astype(jnp.bfloat16)


    lanes = lax.broadcasted_iota(jnp.int32, (1, 128), 1)
    for dx in range(NX):
        for c in range(2):
            to = (x + dx) % NX * 2 + (core if c == 0 else 1 - core)
            first, second = owner[2 * to], owner[2 * to + 1]
            for kk in range(4):
                even, odd = pattern[2 * kk], pattern[2 * kk + 1]

                def hit(tile_id, slot_id):
                    return jnp.where(tile_id == slot_id, jnp.float32(1), jnp.float32(0))

                masks[dx * 2 + c, pl.ds(2 * kk, 1), :] = jnp.where(lanes < 64, hit(even, first), hit(odd, second))
                masks[dx * 2 + c, pl.ds(2 * kk + 1, 1), :] = jnp.where(lanes < 64, hit(odd, first), hit(even, second))

    pl.semaphore_wait(barrier, len(friends))
    for part in range(2):
        for way in (1, -1):
            meet(part, way).start()

    load.wait()

    def flip_block(i):
        parts = []
        for h in range(2):
            cols = pl.ds(i * 1024 + h * 512, 512)
            turned = lax.dot_general(perm[...], tile[:, cols], (((1,), (1,)), ((), ())), preferred_element_type=jnp.float32)
            parts.append(turned.reshape(64, 8, 512))
        flip[:, pl.ds(i * 16, 16), :] = jnp.concatenate(parts, axis=1).astype(jnp.bfloat16)

    def compute(group, n):
        lo, hi = GROUPS[group]
        blocks = ORDER[lo:hi]
        left = jnp.concatenate([gath[dz].reshape(NY * ROWS, TT) for dz in blocks], axis=0)
        if n < 2:
            right = tile[pl.ds(n * 256, 256), :]
            got = lax.dot_general(left, right, (((1,), (1,)), ((), ())), preferred_element_type=jnp.float32)
        else:
            right = flip[:, :, pl.ds((n - 2) * 256, 256)].reshape(TT, 256)
            got = jnp.dot(left, right, preferred_element_type=jnp.float32)
        for i in range(len(blocks)):
            acc[2 * (lo + i) + n // 2, :, pl.ds(n % 2 * 256, 256)] = got[i * 32:(i + 1) * 32]

    def spread(group):
        lo, hi = GROUPS[group]
        for position in range(2 * lo, 2 * hi):
            straight = [acc[position, :, pl.ds(128 * kk, 128)] for kk in range(4)]
            turned = [pltpu.roll(v, 64, 1) for v in straight]
            for dx in range(NX):
                for c in range(2):
                    total = jnp.zeros((32, 128), jnp.float32)
                    for kk in range(4):
                        total += straight[kk] * masks[dx * 2 + c, pl.ds(2 * kk, 1), :]
                        total += turned[kk] * masks[dx * 2 + c, pl.ds(2 * kk + 1, 1), :]
                    if c == 0:
                        one_own[dx, position] = total
                    else:
                        one_out[dx, position] = total.astype(jnp.bfloat16)
        stage_one(group).start()

    def middle(group):
        lo, hi = GROUPS[group]
        stage_one(group).wait_recv()
        for dx in (1, 2, 3, 0):
            for position in range(2 * lo, 2 * hi):
                total = one_own[dx, position] + one_in[dx, position].astype(jnp.float32)
                if dx == 0:
                    one_own[0, position] = total
                else:
                    two_out[dx - 1, position] = total.astype(jnp.bfloat16)
            if dx:
                stage_two(group, dx).start()

    def finish(group):
        lo, hi = GROUPS[group]
        for dx in range(1, NX):
            stage_two(group, dx).wait_recv()
        for position in range(2 * lo, 2 * hi):
            total = one_own[0, position]
            for dx in range(1, NX):
                total += two_in[dx - 1, position].astype(jnp.float32)
            final[position] = total.reshape(NY, ROWS, 128).astype(jnp.bfloat16)
        for index in range(lo, hi):
            for side in (1, -1):
                for dy in (2, 1, 3, 0):
                    if (ORDER[index] + 4 * side) % NZ or dy:
                        deliver(index, side, dy).start()
                    else:
                        landed[pair] = final[2 * index + upper(0), 0]

    def add_up(cols):
        gath[0, 0, :, cols] = (met[0, :, cols].astype(jnp.float32) + met[1, :, cols].astype(jnp.float32)).astype(jnp.bfloat16)

    def pass_b(*blocks):
        for dz in blocks:
            for way in (1, -1):
                y_b(dz, way).start()

    def relay_b(*blocks):
        for dz in blocks:
            for way in (1, -1):
                y_b(dz, way).wait_recv()
                y_b2(dz, way).start()

    def whole_b(*blocks):
        for dz in blocks:
            for way in (1, -1):
                y_b2(dz, way).wait_recv()

    def ends_a(dy):
        return 1 if dy < 2 else -1

    def send_a(dy):
        for far in (2, 1):
            for way in (1, -1):
                z_a(far, way, dy).start()

    def relay_a(*dys):
        for dy in dys:
            for way in (1, -1):
                z_a(2, way, dy).wait_recv()
                if way == ends_a(dy):
                    z_a(4, way, dy).start()
                z_a(3, way, dy).start()

    def whole_a(far):
        for dy in range(NY):
            for way in (1, -1) if far < 4 else (ends_a(dy),):
                z_a(far, way, dy).wait_recv()

    for i in range(3):
        flip_block(i)

    for way in (1, -1):
        meet(0, way).wait_recv()
    add_up(ACOLS)
    for way in (1, -1, 2):
        y_a(way).start()
    send_a(0)
    for way in (1, -1):
        meet(1, way).wait_recv()
    add_up(BCOLS)
    for way in (1, -1):
        z_b(2, way).start()
        z_b(1, way).start()
    pass_b(0)
    for way in (1, -1, 2):
        y_a(way).wait_recv()
        send_a(-way % NY)

    flip_block(3)
    for way in (1, -1):
        z_b(1, way).wait_recv()
    pass_b(1, -1)
    relay_a(0)
    for way in (1, -1):
        z_b(2, way).wait_recv()
        z_b(4, way).start()
        z_b(3, way).start()
    relay_b(0)
    pass_b(2, -2)
    relay_a(3, 1, 2)
    whole_b(0)
    compute(0, 0)
    compute(0, 1)
    relay_b(1, -1)
    for way in (1, -1):
        z_b(4, way).wait_recv()
        z_b(3, way).wait_recv()
    pass_b(4, 3, -3)
    compute(0, 2)
    compute(0, 3)
    relay_b(2, -2)
    spread(0)
    whole_a(1)
    whole_b(1, -1)
    compute(1, 0)
    compute(1, 1)
    relay_b(4, 3, -3)
    compute(1, 2)
    compute(1, 3)
    spread(1)
    middle(0)
    whole_b(2, -2)
    for n in range(4):
        compute(2, n)
    spread(2)
    middle(1)
    finish(0)
    middle(2)
    whole_a(3)
    whole_a(4)
    whole_b(4, 3, -3)
    for n in range(4):
        compute(3, n)
    spread(3)
    finish(1)
    middle(3)
    finish(2)
    finish(3)

    for index in range(NB):
        for side in (1, -1):
            for dy in range(NY):
                if (ORDER[index] + 4 * side) % NZ or dy:
                    deliver(index, side, dy).wait_recv()

    natural = jnp.zeros((ROWS, 1), jnp.int32)
    for r in range(ROWS):
        natural = jnp.where(rows_iota == r, place[r], natural)
    for m in range(32):
        blocks = []
        for j in (2 * m, 2 * m + 1):
            found = landed[j].astype(jnp.float32)
            picked = jnp.zeros((ROWS, 128), jnp.float32)
            for i in range(ROWS):
                picked = jnp.where(natural == i, found[i:i + 1, :], picked)
            blocks.append(picked)
        cols = pl.ds(128 * m, 128)
        out[0, :, cols] = jnp.where(low, blocks[0], pltpu.roll(blocks[1], 64, 1)).astype(jnp.bfloat16)
        out[1, :, cols] = jnp.where(low, pltpu.roll(blocks[0], 64, 1), blocks[1]).astype(jnp.bfloat16)

    for one in table.values():
        one.wait_send()


MESSAGES = 4 + 8 + 28 + 16 + 16 + 3 + 4 + 12 + 63


def shards(amplitudes, partner, integrals, pattern, owner):
    plain = amplitudes.reshape(ROWS, TT)
    vmem = pl.BlockSpec(memory_space=pltpu.VMEM)
    smem = pl.BlockSpec(memory_space=pltpu.SMEM)
    result = pl.pallas_call(
        kernel,
        out_shape=jax.ShapeDtypeStruct((2, ROWS, TT), jnp.bfloat16),
        in_specs=[vmem, pl.BlockSpec(memory_space=pl.ANY), smem, smem, smem],
        out_specs=vmem,
        scratch_shapes=[
            pltpu.VMEM((ROWS, TT), jnp.bfloat16),
            pltpu.VMEM((2, ROWS, TT), jnp.bfloat16),
            pltpu.VMEM((NB, NY, ROWS, TT), jnp.bfloat16),
            pltpu.VMEM((512, TT), jnp.bfloat16),
            pltpu.VMEM((64, 64, 512), jnp.bfloat16),
            pltpu.VMEM((NZ, 32, 512), jnp.float32),
            pltpu.VMEM((512, 512), jnp.bfloat16),
            pltpu.VMEM((8, 8, 128), jnp.float32),
            pltpu.VMEM((NX, NZ, 32, 128), jnp.bfloat16),
            pltpu.VMEM((NX, NZ, 32, 128), jnp.float32),
            pltpu.VMEM((NX, NZ, 32, 128), jnp.bfloat16),
            pltpu.VMEM((NX - 1, NZ, 32, 128), jnp.bfloat16),
            pltpu.VMEM((NX - 1, NZ, 32, 128), jnp.bfloat16),
            pltpu.VMEM((NZ, NY, ROWS, 128), jnp.bfloat16),
            pltpu.VMEM((NZ * NY, ROWS, 128), jnp.bfloat16),
            pltpu.SemaphoreType.DMA,
            pltpu.SemaphoreType.DMA((MESSAGES,)),
            pltpu.SemaphoreType.DMA((MESSAGES,)),
        ],
        compiler_params=pltpu.CompilerParams(collective_id=0, has_side_effects=True, vmem_limit_bytes=60 * 2**20),
    )(plain, integrals.reshape(512, TT), partner, pattern, owner)
    return jnp.swapaxes(result, 0, 1)


def solution(mesh):
    return jax.shard_map(
        shards,
        mesh=mesh,
        in_specs=(P("pair", "virt", None), P("pair"), P("virt", "pair", None), P("virt"), P()),
        out_specs=P("pair", "virt", None),
        check_vma=False,
    )
```

```python
import jax
import jax.numpy as jnp
from jax import lax
from jax.experimental import pallas as pl
from jax.experimental.pallas import tpu as pltpu
from jax.sharding import PartitionSpec as P

MESH = pl.DeviceIdType.MESH
NZ, NY, NX = 16, 4, 4
NB = NZ // 2
ROWS = 8
TT = 4096
CUT = 1536
HALF = (TT - CUT) // 2
ORDER = (0, 1, 7, 2, 6, 3, 5, 4)
GROUPS = ((0, 1), (1, 3), (3, 5), (5, 8))

ACOLS = pl.ds(0, CUT)
BCOLS = pl.ds(CUT, TT - CUT)
BHALF = {1: pl.ds(CUT, HALF), -1: pl.ds(CUT + HALF, HALF)}


def kernel(amp, ints, partner, pattern, owner, out, mine, met, gath, tile, flip, acc, perm, masks,
           one_out, one_own, one_in, two_out, two_in, final, landed, load_sem, send, recv):
    pair = lax.axis_index("pair")
    virt = lax.axis_index("virt")
    z, y = pair // NY, pair % NY
    x, core = virt // 2, virt % 2

    def at(dz, dy):
        return ((z + (dz % NZ)) % NZ * NY + (y + (dy % NY)) % NY, virt)

    def beside(dx, swap):
        return (pair, (x + dx) % NX * 2 + (1 - core if swap else core))

    load = pltpu.make_async_copy(ints, tile, load_sem)
    load.start()

    table = {}

    def message(key, src, dst, device):
        if key not in table:
            slot = len(table)
            table[key] = pltpu.make_async_remote_copy(
                src_ref=src, dst_ref=dst, send_sem=send.at[slot], recv_sem=recv.at[slot],
                device_id=device, device_id_type=MESH)
        return table[key]

    def meet(part, way):
        cols = ACOLS if part == 0 else BCOLS
        return message(("meet", part, way), mine.at[:, cols], met.at[(1 - way) // 2, :, cols], at(4 * way, 0))

    def z_b(far, way):
        if far < 3:
            return message(("zb", far, way), gath.at[0, 0, :, BCOLS], gath.at[(-way * far) % NB, 0, :, BCOLS], at(way * far, 0))
        cols = BCOLS if far == 3 else BHALF[way]
        return message(("zb", far, way), gath.at[(-way * 2) % NB, 0, :, cols],
                       gath.at[(-way * far) % NB, 0, :, cols], at(way * (far - 2), 0))

    def z_a(far, way, dy):
        origin = 0 if far < 3 else (-way * 2) % NB
        return message(("za", far, way, dy), gath.at[origin, dy, :, ACOLS],
                       gath.at[(-way * far) % NB, dy, :, ACOLS], at(way * (far if far < 3 else far - 2), 0))

    def y_b(dz, way):
        dz %= NB
        return message(("yb", dz, way), gath.at[dz, 0, :, BCOLS], gath.at[dz, -way % NY, :, BCOLS], at(0, way))

    def y_b2(dz, way):
        dz %= NB
        return message(("yb2", dz, way), gath.at[dz, -way % NY, :, BHALF[way]], gath.at[dz, 2, :, BHALF[way]], at(0, way))

    def y_a(way):
        return message(("ya", way), gath.at[0, 0, :, ACOLS], gath.at[0, -way % NY, :, ACOLS], at(0, way))

    def stage_one(group):
        lo, hi = GROUPS[group]
        return message(("one", group), one_out.at[:, 2 * lo:2 * hi], one_in.at[:, 2 * lo:2 * hi], beside(0, True))

    def stage_two(group, dx):
        lo, hi = GROUPS[group]
        return message(("two", group, dx), two_out.at[dx - 1, 2 * lo:2 * hi], two_in.at[dx - 1, 2 * lo:2 * hi], beside(dx, False))

    def upper(dz):
        return (z + (dz % NZ)) % NZ // NB

    def deliver(index, side, dy):
        dz = ORDER[index] + 4 * side
        return message(("out", index, side, dy), final.at[2 * index + upper(dz), dy], landed.at[pair], at(dz, dy))

    barrier = pltpu.get_barrier_semaphore()
    friends = [at(4, 0), at(-4, 0), at(1, 0), at(-1, 0), at(2, 0), at(-2, 0), at(0, 1), at(0, -1), at(0, 2),
               beside(0, True), beside(1, False), beside(2, False), beside(3, False)]
    for friend in friends:
        pl.semaphore_signal(barrier, inc=1, device_id=friend, device_id_type=MESH)

    row = lax.broadcasted_iota(jnp.int32, (512, 512), 0)
    col = lax.broadcasted_iota(jnp.int32, (512, 512), 1)
    perm[...] = jnp.where(col == (row % 8) * 64 + row // 8, 1.0, 0.0).astype(jnp.bfloat16)
    rows_iota = lax.broadcasted_iota(jnp.int32, (ROWS, 1), 0)
    lower = z < NB
    place = [jnp.where(lower, r, partner[r] % ROWS) for r in range(ROWS)]
    plain = amp[...].astype(jnp.float32)
    sorted_rows = jnp.zeros((ROWS, TT), jnp.float32)
    for r in range(ROWS):
        sorted_rows = jnp.where(rows_iota == place[r], plain[r:r + 1, :], sorted_rows)

    def exchange(value, order):
        return lax.dot_general(value.astype(jnp.bfloat16), order, (((1,), (1,)), ((), ())), preferred_element_type=jnp.float32)

    low = lax.broadcasted_iota(jnp.int32, (ROWS, 128), 1) < 64
    stacked = jnp.concatenate([sorted_rows[:, 512 * b:512 * (b + 1)] for b in range(8)], axis=0)
    once = exchange(stacked, perm[...])
    regrouped = []
    for e in range(8):
        pieces = []
        for k in range(4):
            first = once[16 * k:16 * k + 8, 128 * (e // 2):128 * (e // 2 + 1)]
            second = once[16 * k + 8:16 * k + 16, 128 * (e // 2):128 * (e // 2 + 1)]
            if e % 2:
                pieces.append(jnp.where(low, pltpu.roll(first, 64, 1), second))
            else:
                pieces.append(jnp.where(low, first, pltpu.roll(second, 64, 1)))
        regrouped.append(jnp.concatenate(pieces, axis=1))
    second_order = jnp.where(col == row % 64 // 8 * 64 + row // 64 * 8 + row % 8, 1.0, 0.0).astype(jnp.bfloat16)
    twice = exchange(jnp.concatenate(regrouped, axis=0), second_order)
    for e in range(8):
        cols = pl.ds(512 * e, 512)
        mine[:, cols] = jnp.where(lower, sorted_rows[:, 512 * e:512 * (e + 1)], twice[8 * e:8 * (e + 1)]).astype(jnp.bfloat16)


    lanes = lax.broadcasted_iota(jnp.int32, (1, 128), 1)
    for dx in range(NX):
        for c in range(2):
            to = (x + dx) % NX * 2 + (core if c == 0 else 1 - core)
            first, second = owner[2 * to], owner[2 * to + 1]
            for kk in range(4):
                even, odd = pattern[2 * kk], pattern[2 * kk + 1]

                def hit(tile_id, slot_id):
                    return jnp.where(tile_id == slot_id, jnp.float32(1), jnp.float32(0))

                masks[dx * 2 + c, pl.ds(2 * kk, 1), :] = jnp.where(lanes < 64, hit(even, first), hit(odd, second))
                masks[dx * 2 + c, pl.ds(2 * kk + 1, 1), :] = jnp.where(lanes < 64, hit(odd, first), hit(even, second))

    pl.semaphore_wait(barrier, len(friends))
    for part in range(2):
        for way in (1, -1):
            meet(part, way).start()

    load.wait()

    def flip_block(i):
        parts = []
        for h in range(2):
            cols = pl.ds(i * 1024 + h * 512, 512)
            turned = lax.dot_general(perm[...], tile[:, cols], (((1,), (1,)), ((), ())), preferred_element_type=jnp.float32)
            parts.append(turned.reshape(64, 8, 512))
        flip[:, pl.ds(i * 16, 16), :] = jnp.concatenate(parts, axis=1).astype(jnp.bfloat16)

    def compute(group, n):
        lo, hi = GROUPS[group]
        blocks = ORDER[lo:hi]
        left = jnp.concatenate([gath[dz].reshape(NY * ROWS, TT) for dz in blocks], axis=0)
        if n < 2:
            right = tile[pl.ds(n * 256, 256), :]
            got = lax.dot_general(left, right, (((1,), (1,)), ((), ())), preferred_element_type=jnp.float32)
        else:
            right = flip[:, :, pl.ds((n - 2) * 256, 256)].reshape(TT, 256)
            got = jnp.dot(left, right, preferred_element_type=jnp.float32)
        for i in range(len(blocks)):
            acc[2 * (lo + i) + n // 2, :, pl.ds(n % 2 * 256, 256)] = got[i * 32:(i + 1) * 32]

    def spread(group):
        lo, hi = GROUPS[group]
        for position in range(2 * lo, 2 * hi):
            straight = [acc[position, :, pl.ds(128 * kk, 128)] for kk in range(4)]
            turned = [pltpu.roll(v, 64, 1) for v in straight]
            for dx in range(NX):
                for c in range(2):
                    total = jnp.zeros((32, 128), jnp.float32)
                    for kk in range(4):
                        total += straight[kk] * masks[dx * 2 + c, pl.ds(2 * kk, 1), :]
                        total += turned[kk] * masks[dx * 2 + c, pl.ds(2 * kk + 1, 1), :]
                    if c == 0:
                        one_own[dx, position] = total
                    else:
                        one_out[dx, position] = total.astype(jnp.bfloat16)
        stage_one(group).start()

    def middle(group):
        lo, hi = GROUPS[group]
        stage_one(group).wait_recv()
        for dx in (1, 2, 3, 0):
            for position in range(2 * lo, 2 * hi):
                total = one_own[dx, position] + one_in[dx, position].astype(jnp.float32)
                if dx == 0:
                    one_own[0, position] = total
                else:
                    two_out[dx - 1, position] = total.astype(jnp.bfloat16)
            if dx:
                stage_two(group, dx).start()

    def finish(group):
        lo, hi = GROUPS[group]
        for dx in range(1, NX):
            stage_two(group, dx).wait_recv()
        for position in range(2 * lo, 2 * hi):
            total = one_own[0, position]
            for dx in range(1, NX):
                total += two_in[dx - 1, position].astype(jnp.float32)
            final[position] = total.reshape(NY, ROWS, 128).astype(jnp.bfloat16)
        for index in range(lo, hi):
            for side in (1, -1):
                for dy in (2, 1, 3, 0):
                    if (ORDER[index] + 4 * side) % NZ or dy:
                        deliver(index, side, dy).start()
                    else:
                        landed[pair] = final[2 * index + upper(0), 0]

    def add_up(cols):
        gath[0, 0, :, cols] = (met[0, :, cols].astype(jnp.float32) + met[1, :, cols].astype(jnp.float32)).astype(jnp.bfloat16)

    def pass_b(*blocks):
        for dz in blocks:
            for way in (1, -1):
                y_b(dz, way).start()

    def relay_b(*blocks):
        for dz in blocks:
            for way in (1, -1):
                y_b(dz, way).wait_recv()
                y_b2(dz, way).start()

    def whole_b(*blocks):
        for dz in blocks:
            for way in (1, -1):
                y_b2(dz, way).wait_recv()

    def ends_a(dy):
        return 1 if dy < 2 else -1

    def send_a(dy):
        for far in (2, 1):
            for way in (1, -1):
                z_a(far, way, dy).start()

    def relay_a(*dys):
        for dy in dys:
            for way in (1, -1):
                z_a(2, way, dy).wait_recv()
                if way == ends_a(dy):
                    z_a(4, way, dy).start()
                z_a(3, way, dy).start()

    def whole_a(far):
        for dy in range(NY):
            for way in (1, -1) if far < 4 else (ends_a(dy),):
                z_a(far, way, dy).wait_recv()

    for i in range(3):
        flip_block(i)

    for way in (1, -1):
        meet(0, way).wait_recv()
    add_up(ACOLS)
    for way in (1, -1, 2):
        y_a(way).start()
    send_a(0)
    for way in (1, -1):
        meet(1, way).wait_recv()
    add_up(BCOLS)
    for way in (1, -1):
        z_b(2, way).start()
        z_b(1, way).start()
    pass_b(0)
    for way in (1, -1, 2):
        y_a(way).wait_recv()
        send_a(-way % NY)

    flip_block(3)
    for way in (1, -1):
        z_b(1, way).wait_recv()
    pass_b(1, -1)
    relay_a(0)
    for way in (1, -1):
        z_b(2, way).wait_recv()
        z_b(3, way).start()
        z_b(4, way).start()
    relay_b(0)
    pass_b(2, -2)
    relay_a(3, 1, 2)
    whole_b(0)
    compute(0, 0)
    compute(0, 1)
    relay_b(1, -1)
    for way in (1, -1):
        z_b(3, way).wait_recv()
    pass_b(3, -3)
    for way in (1, -1):
        z_b(4, way).wait_recv()
    pass_b(4)
    compute(0, 2)
    compute(0, 3)
    relay_b(2, -2)
    spread(0)
    whole_a(1)
    whole_b(1, -1)
    compute(1, 0)
    compute(1, 1)
    relay_b(3, -3, 4)
    compute(1, 2)
    compute(1, 3)
    spread(1)
    middle(0)
    whole_b(2, -2)
    for n in range(4):
        compute(2, n)
    spread(2)
    middle(1)
    finish(0)
    middle(2)
    whole_a(3)
    whole_a(4)
    whole_b(4, 3, -3)
    for n in range(4):
        compute(3, n)
    spread(3)
    finish(1)
    middle(3)
    finish(2)
    finish(3)

    for index in range(NB):
        for side in (1, -1):
            for dy in range(NY):
                if (ORDER[index] + 4 * side) % NZ or dy:
                    deliver(index, side, dy).wait_recv()

    natural = jnp.zeros((ROWS, 1), jnp.int32)
    for r in range(ROWS):
        natural = jnp.where(rows_iota == r, place[r], natural)
    for m in range(32):
        blocks = []
        for j in (2 * m, 2 * m + 1):
            found = landed[j].astype(jnp.float32)
            picked = jnp.zeros((ROWS, 128), jnp.float32)
            for i in range(ROWS):
                picked = jnp.where(natural == i, found[i:i + 1, :], picked)
            blocks.append(picked)
        cols = pl.ds(128 * m, 128)
        out[0, :, cols] = jnp.where(low, blocks[0], pltpu.roll(blocks[1], 64, 1)).astype(jnp.bfloat16)
        out[1, :, cols] = jnp.where(low, pltpu.roll(blocks[0], 64, 1), blocks[1]).astype(jnp.bfloat16)

    for one in table.values():
        one.wait_send()


MESSAGES = 4 + 8 + 28 + 16 + 16 + 3 + 4 + 12 + 63


def shards(amplitudes, partner, integrals, pattern, owner):
    plain = amplitudes.reshape(ROWS, TT)
    vmem = pl.BlockSpec(memory_space=pltpu.VMEM)
    smem = pl.BlockSpec(memory_space=pltpu.SMEM)
    result = pl.pallas_call(
        kernel,
        out_shape=jax.ShapeDtypeStruct((2, ROWS, TT), jnp.bfloat16),
        in_specs=[vmem, pl.BlockSpec(memory_space=pl.ANY), smem, smem, smem],
        out_specs=vmem,
        scratch_shapes=[
            pltpu.VMEM((ROWS, TT), jnp.bfloat16),
            pltpu.VMEM((2, ROWS, TT), jnp.bfloat16),
            pltpu.VMEM((NB, NY, ROWS, TT), jnp.bfloat16),
            pltpu.VMEM((512, TT), jnp.bfloat16),
            pltpu.VMEM((64, 64, 512), jnp.bfloat16),
            pltpu.VMEM((NZ, 32, 512), jnp.float32),
            pltpu.VMEM((512, 512), jnp.bfloat16),
            pltpu.VMEM((8, 8, 128), jnp.float32),
            pltpu.VMEM((NX, NZ, 32, 128), jnp.bfloat16),
            pltpu.VMEM((NX, NZ, 32, 128), jnp.float32),
            pltpu.VMEM((NX, NZ, 32, 128), jnp.bfloat16),
            pltpu.VMEM((NX - 1, NZ, 32, 128), jnp.bfloat16),
            pltpu.VMEM((NX - 1, NZ, 32, 128), jnp.bfloat16),
            pltpu.VMEM((NZ, NY, ROWS, 128), jnp.bfloat16),
            pltpu.VMEM((NZ * NY, ROWS, 128), jnp.bfloat16),
            pltpu.SemaphoreType.DMA,
            pltpu.SemaphoreType.DMA((MESSAGES,)),
            pltpu.SemaphoreType.DMA((MESSAGES,)),
        ],
        compiler_params=pltpu.CompilerParams(collective_id=0, has_side_effects=True, vmem_limit_bytes=60 * 2**20),
    )(plain, integrals.reshape(512, TT), partner, pattern, owner)
    return jnp.swapaxes(result, 0, 1)


def solution(mesh):
    return jax.shard_map(
        shards,
        mesh=mesh,
        in_specs=(P("pair", "virt", None), P("pair"), P("virt", "pair", None), P("virt"), P()),
        out_specs=P("pair", "virt", None),
        check_vma=False,
    )
```
